32 devices in a mesh: row: 8 (over y, x, core), col: 4 (over z).
Axes of the slice: x: 2, y: 2, z: 4, core: 2. Of those that a mesh axis runs over, the one named last changes fastest.
Arguments:
- classes: int32 [128, 64], P('row', 'col'), may hold values from 0 to 15
- features: bfloat16 [128, 64, 128], P('row', 'col'), may hold values from -6 to 6
- cotangent: bfloat16 [128, 64, 128], P('row', 'col'), may hold values from -6 to 6
- table: float32 [16, 128], replicated, may hold values from -6 to 6
- norm_gain: float32 [128], replicated, may hold values from 0.5 to 1.5
- in_weight: bfloat16 [128, 512], replicated, may hold values from -0.5 to 0.5
- scan_weight: bfloat16 [256, 160], replicated, may hold values from -0.375 to 0.375
- step_weight: float32 [4, 8, 256], replicated, may hold values from -2 to 2
- step_bias: float32 [4, 256], replicated, may hold values from -6 to -2.5
- decay_log: float32 [4, 16, 256], replicated, may hold values from -4 to 2
- skip_gain: float32 [4, 256], replicated, may hold values from 0.5 to 1.5
- output_gain: float32 [256], replicated, may hold values from 0.5 to 1.5
- output_weight: bfloat16 [256, 128], replicated, may hold values from -0.375 to 0.375
Outputs:
- feature_grad: bfloat16 [128, 64, 128], P('row', 'col')
- in_weight_grad: float32 [128, 512], replicated
- scan_weight_grad: float32 [256, 160], replicated
- step_weight_grad: float32 [4, 8, 256], replicated
- step_bias_grad: float32 [4, 256], replicated
- decay_log_grad: float32 [4, 16, 256], replicated
- skip_gain_grad: float32 [4, 256], replicated
- norm_gain_grad: float32 [128], replicated
- output_gain_grad: float32 [256], replicated
- output_weight_grad: float32 [256, 128], replicated
The draws below stay inside these ranges and needn't reach their ends.
All inputs are finite; a program needn't handle non-finite values.
Results may differ from the reference program's by a relative error of at most 0.0076.
Values sent between devices are 32-bit elements; how exact they have to be, the bound alone decides.
A program may use at most 320 MiB of HBM per device.

```python
import math
import jax
import jax.numpy as jnp
import numpy as np
from jax import lax

D = 128
E = 256
STATE = 16
RANK = 8
CLASSES = 16
TILE = 16
HEIGHT = 128
WIDTH = 64
TOKENS = 8192


def touch_ends(drawn, rng, least, high):
    index_at = [jax.random.randint(jax.random.fold_in(rng, axis), (), 0, length) for axis, length in enumerate(drawn.shape)]
    widest = drawn.shape.index(max(drawn.shape))
    beside = index_at[:widest] + [(index_at[widest] + 1) % drawn.shape[widest]] + index_at[widest + 1:]
    return drawn.at[tuple(index_at)].set(least).at[tuple(beside)].set(high)


def shard_levels(rng, shape, shards, low, largest):
    def one(position, parts):
        steps = jax.random.uniform(jax.random.fold_in(jax.random.fold_in(rng, 6), position), (parts,), jnp.float32, low / len(shards), largest / len(shards))
        return jnp.repeat(jnp.exp(steps), shape[position] // parts).reshape((-1,) + (1,) * (len(shape) - position - 1))

    level = one(*shards[0])
    for cut in shards[1:]:
        level = level * one(*cut)
    return level


def cumulative_ranks(amount, skew):
    portions = [(1 << 20) // math.isqrt(rank ** skew) + 1 for rank in range(1, amount + 1)]
    scale = 1 + sum(portions) // (1 << 30)
    return np.cumsum(np.array([max(1, weight // scale) for weight in portions]))


def skewed_ids(own_key, shape, count, lean):
    table = cumulative_ranks(count, lean)
    lot = jax.random.randint(jax.random.fold_in(own_key, 1), shape, 0, int(table[count - 1]))
    grade = jnp.searchsorted(jnp.asarray(table, jnp.int32), lot, side="right")
    return jax.random.permutation(jax.random.fold_in(own_key, 2), count)[grade].astype(jnp.int32)


def normal_values(stream_key, extent, scale, limit, split=(), held_as=jnp.bfloat16):
    values = jax.random.normal(stream_key, extent, jnp.float32) * scale
    if len(split) > 0:
        values = shard_levels(stream_key, extent, split, -0.22, 0.18) * values
    return jnp.clip(values, min=-limit, max=limit).astype(held_as)


def setup_inputs(seed: int = 0) -> dict:
    arg_keys = jax.random.split(jax.random.key(seed), 14)
    classes = touch_ends(skewed_ids(arg_keys[0], (HEIGHT, WIDTH), CLASSES, 2), jax.random.fold_in(arg_keys[0], 3), 0, CLASSES - 1).astype(jnp.int32)
    features = normal_values(arg_keys[1], (HEIGHT, WIDTH, D), 1.0, 6.0, ((0, 8), (1, 4)))
    cotangent = normal_values(arg_keys[2], (HEIGHT, WIDTH, D), 1.0, 6.0, ((0, 8), (1, 4)))
    table = normal_values(arg_keys[3], (CLASSES, D), 1.0, 6.0, (), jnp.float32)
    norm_gain = jnp.clip(1.0 + 0.1 * jax.random.normal(arg_keys[4], (D,), jnp.float32), 0.5, 1.5)
    in_weight = normal_values(arg_keys[5], (D, 2 * E), D ** -0.5, 0.5)
    scan_weight = normal_values(arg_keys[6], (E, 4 * (RANK + 2 * STATE)), E ** -0.5, 0.375)
    step_weight = normal_values(arg_keys[7], (4, RANK, E), RANK ** -0.5, 2.0, (), jnp.float32)
    step_bias = jnp.clip(jax.random.uniform(arg_keys[8], (4, E), jnp.float32, -6.0, -2.5), -6.0, -2.5)
    decay_log = jnp.clip(jax.random.uniform(arg_keys[9], (4, STATE, E), jnp.float32, -4.0, 2.0), -4.0, 2.0)
    skip_gain = jnp.clip(jax.random.uniform(arg_keys[10], (4, E), jnp.float32, 0.5, 1.5), 0.5, 1.5)
    output_gain = jnp.clip(1.0 + 0.1 * jax.random.normal(arg_keys[11], (E,), jnp.float32), 0.5, 1.5)
    output_weight = normal_values(arg_keys[12], (E, D), E ** -0.5, 0.375)
    return {"classes": classes, "features": features, "cotangent": cotangent, "table": table, "norm_gain": norm_gain, "in_weight": in_weight, "scan_weight": scan_weight, "step_weight": step_weight, "step_bias": step_bias, "decay_log": decay_log, "skip_gain": skip_gain, "output_gain": output_gain, "output_weight": output_weight}


EPS = 1e-05
HIGHEST = lax.Precision.HIGHEST

def layer_norm(rows, gain):
    average = lax.optimization_barrier(jnp.mean(rows, axis=-1, keepdims=True))
    centred = rows - average
    spread = lax.optimization_barrier(jnp.mean(centred * centred, axis=-1, keepdims=True))
    return centred * lax.rsqrt(spread + EPS) * gain

def silu_slope(before):
    sigma = jax.nn.sigmoid(before)
    return sigma * (1.0 + before * (1.0 - sigma))

def embed(features, classes, table):
    labels = jnp.arange(table.shape[0], dtype=jnp.int32)
    onehot = (classes[..., None] == labels).astype(jnp.float32)
    lookup = jnp.einsum('hwk,kd->hwd', onehot, table.astype(jnp.float32), precision=HIGHEST)
    return features.astype(jnp.float32) + lookup

def direction_inputs(projected, step_weight, step_bias):
    rank = step_weight.shape[1]
    group = projected.shape[1] // 4
    states = (group - rank) // 2
    steps, inflow, readout = ([], [], [])
    for direction in range(4):
        first = direction * group
        lowrank = projected[:, first:first + rank]
        before = jnp.dot(lowrank, step_weight[direction], precision=HIGHEST) + step_bias[direction]
        steps.append(jax.nn.softplus(before))
        inflow.append(projected[:, first + rank:first + rank + states])
        readout.append(projected[:, first + rank + states:first + group])
    return (jnp.stack(steps), jnp.stack(inflow), jnp.stack(readout))

def gate_output(total, gate_in, output_gain):
    return layer_norm(total, output_gain) * jax.nn.silu(gate_in)

def to_sequence(grid, direction):
    if direction < 2:
        grid = jnp.transpose(grid, (1, 0, 2))
    if direction % 2 == 1:
        grid = grid[::-1]
    return grid

def from_sequence(lines, direction):
    if direction % 2 == 1:
        lines = lines[::-1]
    if direction < 2:
        lines = jnp.transpose(lines, (1, 0, 2))
    return lines

def scan_lines(values, steps, inflow, readout, rate, skip, start):

    def advance(state, slab):
        value, step, source, probe = slab
        decay = jnp.exp(step[:, None, :] * rate)
        state = decay * state + source[:, :, None] * (step * value)[:, None, :]
        output = jnp.einsum('bn,bne->be', probe, state, precision=HIGHEST) + skip * value
        return (state, output)
    final, outputs = lax.scan(advance, start, (values, steps, inflow, readout))
    return (outputs, final)

def reference(classes, features, cotangent, table, norm_gain, in_weight, scan_weight, step_weight, step_bias, decay_log, skip_gain, output_gain, output_weight):
    height, width, model_width = features.shape
    inner = output_weight.shape[0]
    count = height * width
    grad_scale = float(TOKENS) ** (-0.5)
    embedded = embed(features, classes, table).reshape(count, model_width)
    normed = layer_norm(embedded, norm_gain).astype(jnp.bfloat16)
    mixed = jnp.dot(normed, in_weight, preferred_element_type=jnp.float32)
    values = jax.nn.silu(mixed[:, :inner]).astype(jnp.bfloat16)
    gate_in = mixed[:, inner:]
    projected = jnp.dot(values, scan_weight, preferred_element_type=jnp.float32)
    steps, inflow, readout = direction_inputs(projected, step_weight, step_bias)
    values_wide = values.astype(jnp.float32)

    def lines_of(flat, direction):
        return to_sequence(flat.reshape(height, width, flat.shape[-1]), direction)

    def flat_of(lines, direction):
        return from_sequence(lines, direction).reshape(count, lines.shape[-1])

    def run_lines(line_values, line_steps, line_inflow, line_readout, log_rate, skip):
        rate = -jnp.exp(log_rate)
        blocks = line_values.shape[0] // TILE

        def regroup(array):
            return array.reshape((blocks, TILE) + array.shape[1:])

        def block(state, slab):
            outputs, state = scan_lines(slab[0], slab[1], slab[2], slab[3], rate, skip, state)
            return (state, outputs)
        start = jnp.zeros((line_values.shape[1], rate.shape[0], rate.shape[1]), jnp.float32)
        unused, outputs = lax.scan(jax.checkpoint(block), start, (regroup(line_values), regroup(line_steps), regroup(line_inflow), regroup(line_readout)))
        return outputs.reshape(line_values.shape)
    total = jnp.zeros((count, inner), jnp.float32)
    pulls = []
    for direction in range(4):
        outputs, pull = jax.vjp(run_lines, lines_of(values_wide, direction), lines_of(steps[direction], direction), lines_of(inflow[direction], direction), lines_of(readout[direction], direction), decay_log[direction], skip_gain[direction])
        pulls.append(pull)
        total = total + flat_of(outputs, direction)
    gated = gate_output(total, gate_in, output_gain).astype(jnp.bfloat16)
    upstream = cotangent.reshape(count, model_width)
    output_weight_grad = jnp.dot(gated.T, upstream, preferred_element_type=jnp.float32)
    d_gated = jnp.dot(upstream, output_weight.T, preferred_element_type=jnp.float32)
    unused, gate_pull = jax.vjp(gate_output, total, gate_in, output_gain)
    d_total, d_gate_in, output_gain_grad = gate_pull(d_gated)
    d_values_scan = jnp.zeros((count, inner), jnp.float32)
    d_steps, d_inflow, d_readout, decay_grads, skip_grads = ([], [], [], [], [])
    for direction in range(4):
        grads = pulls[direction](lines_of(d_total, direction))
        d_values_scan = d_values_scan + flat_of(grads[0], direction)
        d_steps.append(flat_of(grads[1], direction))
        d_inflow.append(flat_of(grads[2], direction))
        d_readout.append(flat_of(grads[3], direction))
        decay_grads.append(grads[4])
        skip_grads.append(grads[5])
    unused, input_pull = jax.vjp(direction_inputs, projected, step_weight, step_bias)
    d_projected, step_weight_grad, step_bias_grad = input_pull((jnp.stack(d_steps), jnp.stack(d_inflow), jnp.stack(d_readout)))
    d_projected = d_projected.astype(jnp.bfloat16)
    scan_weight_grad = jnp.dot(values.T, d_projected, preferred_element_type=jnp.float32)
    d_values = jnp.dot(d_projected, scan_weight.T, preferred_element_type=jnp.float32) + d_values_scan
    d_mixed = jnp.concatenate([d_values * silu_slope(mixed[:, :inner]), d_gate_in], axis=1).astype(jnp.bfloat16)
    in_weight_grad = jnp.dot(normed.T, d_mixed, preferred_element_type=jnp.float32)
    d_normed = jnp.dot(d_mixed, in_weight.T, preferred_element_type=jnp.float32)
    unused, norm_pull = jax.vjp(layer_norm, embedded, norm_gain)
    d_embedded, norm_gain_grad = norm_pull(d_normed)
    feature_grad = (upstream.astype(jnp.float32) + d_embedded).astype(jnp.bfloat16).reshape(height, width, model_width)
    return (feature_grad, in_weight_grad * grad_scale, scan_weight_grad * grad_scale, step_weight_grad * grad_scale, step_bias_grad * grad_scale, jnp.stack(decay_grads) * grad_scale, jnp.stack(skip_grads) * grad_scale, norm_gain_grad * grad_scale, output_gain_grad * grad_scale, output_weight_grad * grad_scale)
```

```python
import functools
import math

import jax
import jax.numpy as jnp
from jax import lax
from jax.experimental import pallas as pl
from jax.experimental.pallas import tpu as pltpu
from jax.sharding import PartitionSpec as P

EPS = 1e-05
HIGHEST = lax.Precision.HIGHEST
MESH = pl.DeviceIdType.MESH
LANES = 128
SUB = 8
LOG2E = math.log2(math.e)
VMEM = pl.BlockSpec(memory_space=pltpu.VMEM)
BIG = 60 * 1024 * 1024


def layer_norm(rows, gain):
    average = jnp.mean(rows, axis=-1, keepdims=True)
    centred = rows - average
    spread = jnp.mean(centred * centred, axis=-1, keepdims=True)
    return centred * lax.rsqrt(spread + EPS) * gain


def silu_slope(before):
    sigma = jax.nn.sigmoid(before)
    return sigma * (1.0 + before * (1.0 - sigma))


def embed(features, classes, table):
    labels = jnp.arange(table.shape[0], dtype=jnp.int32)
    onehot = (classes[..., None] == labels).astype(jnp.float32)
    lookup = jnp.einsum("hwk,kd->hwd", onehot, table, precision=HIGHEST)
    return features.astype(jnp.float32) + lookup


def gate_output(total, gate_in, output_gain):
    return layer_norm(total, output_gain) * jax.nn.silu(gate_in)


def greet(axes):
    barrier = pltpu.get_barrier_semaphore()
    partners = 0
    for axis in axes:
        count = lax.axis_size(axis)
        me = lax.axis_index(axis)
        for d in range(1, count):
            pl.semaphore_signal(
                barrier, inc=1, device_id={axis: lax.rem(me + d, count)}, device_id_type=MESH
            )
            partners += 1
    pl.semaphore_wait(barrier, partners)


def exchange_kernel(axes, *refs):
    k = len(axes)
    sources, results, sems = refs[:k], refs[k : 2 * k], refs[2 * k :]
    greet(axes)
    copies = []
    for i, axis in enumerate(axes):
        count = lax.axis_size(axis)
        me = lax.axis_index(axis)
        for d in range(1, count):
            target = lax.rem(me + d, count)
            copy = pltpu.make_async_remote_copy(
                src_ref=sources[i].at[target],
                dst_ref=results[i].at[me],
                send_sem=sems[2 * i].at[d],
                recv_sem=sems[2 * i + 1].at[d],
                device_id={axis: target},
                device_id_type=MESH,
            )
            copy.start()
            copies.append(copy)
    for i, axis in enumerate(axes):
        me = lax.axis_index(axis)
        results[i][me] = sources[i][me]
    for copy in copies:
        copy.wait()


def exchange(arrays, axes, ident):
    scratch = []
    for axis in axes:
        count = lax.axis_size(axis)
        scratch += [pltpu.SemaphoreType.DMA((count,)), pltpu.SemaphoreType.DMA((count,))]
    return pl.pallas_call(
        functools.partial(exchange_kernel, axes),
        out_shape=[jax.ShapeDtypeStruct(a.shape, a.dtype) for a in arrays],
        in_specs=[VMEM] * len(arrays),
        out_specs=[VMEM] * len(arrays),
        scratch_shapes=scratch,
        compiler_params=pltpu.CompilerParams(collective_id=ident, has_side_effects=True),
    )(*arrays)


def reduce_kernel(x_ref, out_ref, first, partial, second, sems):
    rows, cols = lax.axis_size("row"), lax.axis_size("col")
    r, c = lax.axis_index("row"), lax.axis_index("col")
    greet(("row", "col"))

    def spread(axis, source, result, phase):
        count = lax.axis_size(axis)
        me = lax.axis_index(axis)
        copies = []
        for d in range(1, count):
            target = lax.rem(me + d, count)
            copy = pltpu.make_async_remote_copy(
                src_ref=source(target),
                dst_ref=result(me, d),
                send_sem=sems.at[phase, 0, d],
                recv_sem=sems.at[phase, 1, d],
                device_id={axis: target},
                device_id_type=MESH,
            )
            copy.start()
            copies.append(copy)
        for copy in copies:
            copy.wait()

    spread("row", lambda t: x_ref.at[t], lambda me, d: first.at[d - 1], 0)
    acc = x_ref[r]
    for d in range(rows - 1):
        acc = acc + first[d]
    partial[...] = acc
    spread("col", lambda t: partial.at[t], lambda me, d: second.at[d - 1], 1)
    acc = partial[c]
    for d in range(cols - 1):
        acc = acc + second[d]
    out_ref[r, c] = acc
    spread("col", lambda t: out_ref.at[r, c], lambda me, d: out_ref.at[r, me], 2)
    spread("row", lambda t: out_ref.at[r], lambda me, d: out_ref.at[me], 3)


def reduce_all(flat, ident):
    rows, cols = lax.axis_size("row"), lax.axis_size("col")
    part = flat.shape[2:]
    most = max(rows, cols)
    return pl.pallas_call(
        reduce_kernel,
        out_shape=jax.ShapeDtypeStruct(flat.shape, flat.dtype),
        in_specs=[VMEM],
        out_specs=VMEM,
        scratch_shapes=[
            pltpu.VMEM((rows - 1, cols) + part, jnp.float32),
            pltpu.VMEM((cols,) + part, jnp.float32),
            pltpu.VMEM((cols - 1,) + part, jnp.float32),
            pltpu.SemaphoreType.DMA((4, 2, most)),
        ],
        compiler_params=pltpu.CompilerParams(collective_id=ident, has_side_effects=True),
    )(flat)


def half(ref, k, h, t):
    return ref[k, h, pl.ds(t, 1), :]


def fill_lines(v_ref, s_ref, p_ref, wide, sv, steps):
    count = v_ref.shape[0]
    states = wide.shape[2] // count
    for k in range(2):
        for which in range(2):
            for n in range(states):
                col = (2 * k + which) * states + n
                wide[k, which, pl.ds(n, count, stride=states), :] = jnp.broadcast_to(
                    p_ref[:, col : col + 1], (count, LANES)
                )
        for h in range(sv.shape[1]):
            cols = slice(h * LANES, (h + 1) * LANES)
            step = s_ref[k][:, cols]
            steps[k, h] = step
            sv[k, h] = step * v_ref[:, cols]


def walk(lines, tile, blocks, group, start, step):
    def outer(b, carry):
        def inner(j, carry):
            rising = b * (tile * lines) + j
            falling = (blocks - 1 - b) * (tile * lines) + (tile - 1 - j)
            tokens = [[base + line * tile for line in group] for base in (rising, falling)]
            return step(carry, tokens)

        return lax.fori_loop(0, tile, inner, carry, unroll=2)

    return lax.fori_loop(0, blocks, outer, start)


def groups_of(lines):
    size = 2 if lines % 2 == 0 else 1
    return [tuple(range(g, g + size)) for g in range(0, lines, size)]


def fold(ref, k, h, count):
    total = ref[k, h, pl.ds(0, count, stride=SUB), :]
    for s in range(1, SUB):
        total = total + ref[k, h, pl.ds(s, count, stride=SUB), :]
    return total


def forward_kernel(lines, tile, v_ref, s_ref, p_ref, rate_ref, skip_ref, y_ref, wide, sv, steps, out8):
    count = v_ref.shape[0]
    blocks = count // (lines * tile)
    states = wide.shape[2] // count
    eh, nh = sv.shape[1], states // SUB
    fill_lines(v_ref, s_ref, p_ref, wide, sv, steps)
    for group in groups_of(lines):

        def step(carry, tokens, group=group):
            new = []
            i = 0
            for k in range(2):
                for t in tokens[k]:
                    drive = [half(sv, k, h, t) for h in range(eh)]
                    pace = [half(steps, k, h, t) for h in range(eh)]
                    sums = [None] * eh
                    for m in range(nh):
                        at = pl.ds(pl.multiple_of(t * states + m * SUB, SUB), SUB)
                        source = wide[k, 0, at, :]
                        probe = wide[k, 1, at, :]
                        for h in range(eh):
                            rate = rate_ref[k, m * SUB : (m + 1) * SUB, h * LANES : (h + 1) * LANES]
                            state = jnp.exp2(pace[h] * rate) * carry[i] + source * drive[h]
                            i += 1
                            new.append(state)
                            term = probe * state
                            sums[h] = term if sums[h] is None else sums[h] + term
                    for h in range(eh):
                        out8[k, h, pl.ds(pl.multiple_of(t * SUB, SUB), SUB), :] = sums[h]
            return tuple(new)

        zero = jnp.zeros((SUB, LANES), jnp.float32)
        walk(lines, tile, blocks, group, (zero,) * (2 * len(group) * eh * nh), step)
    for h in range(eh):
        cols = slice(h * LANES, (h + 1) * LANES)
        skip = skip_ref[0:1, cols] + skip_ref[1:2, cols]
        y_ref[:, cols] = fold(out8, 0, h, count) + fold(out8, 1, h, count) + skip * v_ref[:, cols]


def backward_kernel(
    lines, tile, v_ref, s_ref, p_ref, rate_ref, skip_ref, g_ref,
    dv_ref, ds_ref, dp_ref, dr_ref,
    wide, sv, steps, up, before, decay, drive8, pace8,
):
    count = v_ref.shape[0]
    blocks = count // (lines * tile)
    states = wide.shape[2] // count
    eh, nh = sv.shape[1], states // SUB
    fill_lines(v_ref, s_ref, p_ref, wide, sv, steps)
    for h in range(eh):
        up[0, h] = g_ref[:, h * LANES : (h + 1) * LANES]
    zero = jnp.zeros((SUB, LANES), jnp.float32)

    def rate_of(k, m, h):
        return rate_ref[k, m * SUB : (m + 1) * SUB, h * LANES : (h + 1) * LANES]

    dr_ref[...] = jnp.zeros_like(dr_ref)
    for group in groups_of(lines):

        def advance(carry, tokens):
            new = []
            i = 0
            for k in range(2):
                for t in tokens[k]:
                    drive = [half(sv, k, h, t) for h in range(eh)]
                    pace = [half(steps, k, h, t) for h in range(eh)]
                    g = [half(up, 0, h, t) for h in range(eh)]
                    for m in range(nh):
                        at = pl.ds(pl.multiple_of(t * states + m * SUB, SUB), SUB)
                        source = wide[k, 0, at, :]
                        total = None
                        for h in range(eh):
                            a = jnp.exp2(pace[h] * rate_of(k, m, h))
                            before[k, h, at, :] = carry[i]
                            decay[k, h, at, :] = a
                            state = a * carry[i] + source * drive[h]
                            i += 1
                            new.append(state)
                            term = g[h] * state
                            total = term if total is None else total + term
                        wide[k, 2, at, :] = total
            return tuple(new)

        def retreat(carry, tokens):
            grads, rates = carry
            rates = list(rates)
            new = []
            i = 0
            for k in range(2):
                for t in tokens[1 - k]:
                    drive = [half(sv, k, h, t) for h in range(eh)]
                    pace = [half(steps, k, h, t) for h in range(eh)]
                    g = [half(up, 0, h, t) for h in range(eh)]
                    dd = [None] * eh
                    dp = [None] * eh
                    for m in range(nh):
                        at = pl.ds(pl.multiple_of(t * states + m * SUB, SUB), SUB)
                        source = wide[k, 0, at, :]
                        probe = wide[k, 1, at, :]
                        total = None
                        for h in range(eh):
                            grad = grads[i] + probe * g[h]
                            i += 1
                            term = grad * drive[h]
                            total = term if total is None else total + term
                            term = grad * source
                            dd[h] = term if dd[h] is None else dd[h] + term
                            carried = decay[k, h, at, :] * grad
                            q = carried * before[k, h, at, :]
                            term = q * rate_of(k, m, h)
                            dp[h] = term if dp[h] is None else dp[h] + term
                            j = (k * nh + m) * eh + h
                            rates[j] = rates[j] + q * pace[h]
                            new.append(carried)
                        wide[k, 3, at, :] = total
                    for h in range(eh):
                        at8 = pl.ds(pl.multiple_of(t * SUB, SUB), SUB)
                        drive8[k, h, at8, :] = dd[h]
                        pace8[k, h, at8, :] = dp[h]
            return (tuple(new), tuple(rates))

        chains = 2 * len(group) * eh * nh
        walk(lines, tile, blocks, group, (zero,) * chains, advance)
        unused, rates = walk(
            lines, tile, blocks, group, ((zero,) * chains, (zero,) * (2 * eh * nh)), retreat
        )
        for k in range(2):
            for m in range(nh):
                for h in range(eh):
                    dr_ref[k, m * SUB : (m + 1) * SUB, h * LANES : (h + 1) * LANES] += rates[
                        (k * nh + m) * eh + h
                    ]
    for h in range(eh):
        cols = slice(h * LANES, (h + 1) * LANES)
        value = v_ref[:, cols]
        dv = (skip_ref[0:1, cols] + skip_ref[1:2, cols]) * g_ref[:, cols]
        for k in range(2):
            drive = fold(drive8, k, h, count)
            dv = dv + drive * steps[k, h]
            ds_ref[k, :, cols] = drive * value + fold(pace8, k, h, count) * (1.0 / LOG2E)
        dv_ref[:, cols] = dv
    for k in range(2):
        for which in range(2):
            for n in range(states):
                col = (2 * k + which) * states + n
                dp_ref[:, col : col + 1] = jnp.sum(
                    wide[k, 3 - which, pl.ds(n, count, stride=states), :], axis=-1, keepdims=True
                )


def scan_scratch(count, states, inner, slots):
    eh = inner // LANES
    return [
        pltpu.VMEM((2, slots, count * states, LANES), jnp.float32),
        pltpu.VMEM((2, eh, count, LANES), jnp.float32),
        pltpu.VMEM((2, eh, count, LANES), jnp.float32),
    ]


def scan_forward(lines, tile, values, steps, flows, rate, skip):
    count, inner = values.shape
    states = rate.shape[1]
    eh = inner // LANES
    return pl.pallas_call(
        functools.partial(forward_kernel, lines, tile),
        out_shape=jax.ShapeDtypeStruct((count, inner), jnp.float32),
        in_specs=[VMEM] * 5,
        out_specs=VMEM,
        scratch_shapes=scan_scratch(count, states, inner, 2)
        + [pltpu.VMEM((2, eh, count * SUB, LANES), jnp.float32)],
        compiler_params=pltpu.CompilerParams(vmem_limit_bytes=BIG),
    )(values, steps, flows, rate, skip)


def scan_backward(lines, tile, values, steps, flows, rate, skip, upstream):
    count, inner = values.shape
    states = rate.shape[1]
    eh = inner // LANES
    return pl.pallas_call(
        functools.partial(backward_kernel, lines, tile),
        out_shape=[
            jax.ShapeDtypeStruct((count, inner), jnp.float32),
            jax.ShapeDtypeStruct((2, count, inner), jnp.float32),
            jax.ShapeDtypeStruct((count, 4 * states), jnp.float32),
            jax.ShapeDtypeStruct((2, states, inner), jnp.float32),
        ],
        in_specs=[VMEM] * 6,
        out_specs=[VMEM] * 4,
        scratch_shapes=scan_scratch(count, states, inner, 4)
        + [
            pltpu.VMEM((1, eh, count, LANES), jnp.float32),
            pltpu.VMEM((2, eh, count * states, LANES), jnp.float32),
            pltpu.VMEM((2, eh, count * states, LANES), jnp.float32),
            pltpu.VMEM((2, eh, count * SUB, LANES), jnp.float32),
            pltpu.VMEM((2, eh, count * SUB, LANES), jnp.float32),
        ],
        compiler_params=pltpu.CompilerParams(vmem_limit_bytes=BIG),
    )(values, steps, flows, rate, skip, upstream)


def local(
    classes, features, cotangent, table, norm_gain, in_weight, scan_weight, step_weight,
    step_bias, decay_log, skip_gain, output_gain, output_weight,
):
    tile_rows, tile_cols, model_width = features.shape
    inner = output_weight.shape[0]
    count = tile_rows * tile_cols
    rows, cols = lax.axis_size("row"), lax.axis_size("col")
    rank = step_weight.shape[1]
    states = decay_log.shape[1]
    group = rank + 2 * states
    grad_scale = float(count * rows * cols) ** (-0.5)
    row_lines, col_lines = tile_rows // cols, tile_cols // rows
    rate = -jnp.exp(decay_log)
    rate2 = rate * LOG2E

    def to_lines(x, ident):
        along = x.reshape(cols, row_lines * tile_cols, x.shape[-1])
        down = jnp.swapaxes(x.reshape(tile_rows, tile_cols, x.shape[-1]), 0, 1)
        down = down.reshape(rows, col_lines * tile_rows, x.shape[-1])
        a, d = exchange((along, down), ("col", "row"), ident)
        return (a.reshape(count, x.shape[-1]), d.reshape(count, x.shape[-1]))

    def from_lines(a, d, ident):
        a, d = exchange(
            (a.reshape(cols, -1, a.shape[-1]), d.reshape(rows, -1, d.shape[-1])), ("col", "row"), ident
        )
        d = jnp.swapaxes(d.reshape(tile_cols, tile_rows, d.shape[-1]), 0, 1)
        return a.reshape(count, -1) + d.reshape(count, -1)

    embedded = embed(features, classes, table).reshape(count, model_width)
    normed = layer_norm(embedded, norm_gain).astype(jnp.bfloat16)
    mixed = jnp.dot(normed, in_weight, preferred_element_type=jnp.float32)
    values = jax.nn.silu(mixed[:, :inner]).astype(jnp.bfloat16)
    gate_in = mixed[:, inner:]
    line_values = to_lines(values.astype(jnp.float32), 1)

    prepared = []
    outputs = []
    for pair in range(2):
        v = line_values[pair]
        dirs = (2 * pair, 2 * pair + 1)
        weight = scan_weight[:, dirs[0] * group : (dirs[1] + 1) * group]
        vb = v.astype(jnp.bfloat16)
        projected = jnp.dot(vb, weight, preferred_element_type=jnp.float32)
        lowrank = [projected[:, i * group : i * group + rank] for i in range(2)]
        before = jnp.stack(
            [
                jnp.dot(lowrank[i], step_weight[dirs[i]], precision=HIGHEST) + step_bias[dirs[i]]
                for i in range(2)
            ]
        )
        steps = jax.nn.softplus(before)
        flows = jnp.concatenate(
            [projected[:, i * group + rank : (i + 1) * group] for i in range(2)], axis=1
        )
        lines, tile = ((row_lines, tile_cols), (col_lines, tile_rows))[pair]
        args = (lines, tile, v, steps, flows, rate2[dirs[0] : dirs[1] + 1], skip_gain[dirs[0] : dirs[1] + 1])
        outputs.append(scan_forward(*args))
        prepared.append((args, vb, weight, lowrank, before))
    total = from_lines(outputs[0], outputs[1], 2)

    gated = gate_output(total, gate_in, output_gain).astype(jnp.bfloat16)
    upstream = cotangent.reshape(count, model_width)
    output_weight_grad = jnp.dot(gated.T, upstream, preferred_element_type=jnp.float32)
    d_gated = jnp.dot(upstream, output_weight.T, preferred_element_type=jnp.float32)
    unused, gate_pull = jax.vjp(gate_output, total, gate_in, output_gain)
    d_total, d_gate_in, output_gain_grad = gate_pull(d_gated)
    line_grads = to_lines(d_total, 3)

    d_lines, scan_grads, stepw_grads, stepb_grads, decay_grads, skip_grads = ([], [], [], [], [], [])
    for pair in range(2):
        args, vb, weight, lowrank, before = prepared[pair]
        g = line_grads[pair]
        dv, ds, dflow, drate = scan_backward(*args, g)
        d_before = ds * jax.nn.sigmoid(before)
        parts = []
        for i in range(2):
            k = 2 * pair + i
            parts.append(jnp.dot(d_before[i], step_weight[k].T, precision=HIGHEST))
            parts.append(dflow[:, i * 2 * states : (i + 1) * 2 * states])
            stepw_grads.append(jnp.dot(lowrank[i].T, d_before[i], precision=HIGHEST))
            stepb_grads.append(jnp.sum(d_before[i], axis=0))
            skip_grads.append(jnp.sum(g * args[2], axis=0))
        decay_grads.append(drate * rate[2 * pair : 2 * pair + 2])
        d_projected = jnp.concatenate(parts, axis=1).astype(jnp.bfloat16)
        scan_grads.append(jnp.dot(vb.T, d_projected, preferred_element_type=jnp.float32))
        d_lines.append(jnp.dot(d_projected, weight.T, preferred_element_type=jnp.float32) + dv)
    d_values = from_lines(d_lines[0], d_lines[1], 4)

    d_mixed = jnp.concatenate([d_values * silu_slope(mixed[:, :inner]), d_gate_in], axis=1).astype(
        jnp.bfloat16
    )
    in_weight_grad = jnp.dot(normed.T, d_mixed, preferred_element_type=jnp.float32)
    d_normed = jnp.dot(d_mixed, in_weight.T, preferred_element_type=jnp.float32)
    unused, norm_pull = jax.vjp(layer_norm, embedded, norm_gain)
    d_embedded, norm_gain_grad = norm_pull(d_normed)
    feature_grad = (
        (upstream.astype(jnp.float32) + d_embedded)
        .astype(jnp.bfloat16)
        .reshape(tile_rows, tile_cols, model_width)
    )
    grads = (
        in_weight_grad,
        jnp.concatenate(scan_grads, axis=1),
        jnp.stack(stepw_grads),
        jnp.stack(stepb_grads),
        jnp.concatenate(decay_grads, axis=0),
        jnp.stack(skip_grads),
        norm_gain_grad,
        output_gain_grad,
        output_weight_grad,
    )
    flat = jnp.concatenate([g.reshape(-1, LANES) for g in grads], axis=0)
    used = flat.shape[0]
    unit = rows * cols * SUB
    padded = -(-used // unit) * unit
    flat = jnp.pad(flat, ((0, padded - used), (0, 0))).reshape(rows, cols, padded // (rows * cols), LANES)
    flat = reduce_all(flat, 5).reshape(padded, LANES) * grad_scale
    summed = []
    place = 0
    for g in grads:
        length = g.size // LANES
        summed.append(flat[place : place + length].reshape(g.shape))
        place += length
    return (feature_grad, *summed)


def solution(mesh):
    in_specs = (P("row", "col"), P("row", "col", None), P("row", "col", None)) + (P(),) * 10
    out_specs = (P("row", "col", None),) + (P(),) * 9
    return jax.shard_map(local, mesh=mesh, in_specs=in_specs, out_specs=out_specs, check_vma=False)
```

```python
import functools
import math

import jax
import jax.numpy as jnp
from jax import lax
from jax.experimental import pallas as pl
from jax.experimental.pallas import tpu as pltpu
from jax.sharding import PartitionSpec as P

EPS = 1e-05
HIGHEST = lax.Precision.HIGHEST
MESH = pl.DeviceIdType.MESH
LANES = 128
SUB = 8
LOG2E = math.log2(math.e)
VMEM = pl.BlockSpec(memory_space=pltpu.VMEM)
BIG = 60 * 1024 * 1024


def layer_norm(rows, gain):
    average = jnp.mean(rows, axis=-1, keepdims=True)
    centred = rows - average
    spread = jnp.mean(centred * centred, axis=-1, keepdims=True)
    return centred * lax.rsqrt(spread + EPS) * gain


def silu_slope(before):
    sigma = jax.nn.sigmoid(before)
    return sigma * (1.0 + before * (1.0 - sigma))


def embed(features, classes, table):
    labels = jnp.arange(table.shape[0], dtype=jnp.int32)
    onehot = (classes[..., None] == labels).astype(jnp.float32)
    lookup = jnp.einsum("hwk,kd->hwd", onehot, table, precision=HIGHEST)
    return features.astype(jnp.float32) + lookup


def gate_output(total, gate_in, output_gain):
    return layer_norm(total, output_gain) * jax.nn.silu(gate_in)


def greet(axes):
    barrier = pltpu.get_barrier_semaphore()
    partners = 0
    for axis in axes:
        count = lax.axis_size(axis)
        me = lax.axis_index(axis)
        for d in range(1, count):
            pl.semaphore_signal(
                barrier, inc=1, device_id={axis: lax.rem(me + d, count)}, device_id_type=MESH
            )
            partners += 1
    pl.semaphore_wait(barrier, partners)


def reduce_kernel(x_ref, out_ref, first, partial, second, sems):
    rows, cols = lax.axis_size("row"), lax.axis_size("col")
    r, c = lax.axis_index("row"), lax.axis_index("col")
    greet(("row", "col"))

    def spread(axis, source, result, phase):
        count = lax.axis_size(axis)
        me = lax.axis_index(axis)
        copies = []
        for d in range(1, count):
            target = lax.rem(me + d, count)
            copy = pltpu.make_async_remote_copy(
                src_ref=source(target),
                dst_ref=result(me, d),
                send_sem=sems.at[phase, 0, d],
                recv_sem=sems.at[phase, 1, d],
                device_id={axis: target},
                device_id_type=MESH,
            )
            copy.start()
            copies.append(copy)
        for copy in copies:
            copy.wait()

    spread("row", lambda t: x_ref.at[t], lambda me, d: first.at[d - 1], 0)
    acc = x_ref[r]
    for d in range(rows - 1):
        acc = acc + first[d]
    partial[...] = acc
    spread("col", lambda t: partial.at[t], lambda me, d: second.at[d - 1], 1)
    acc = partial[c]
    for d in range(cols - 1):
        acc = acc + second[d]
    out_ref[r, c] = acc
    spread("col", lambda t: out_ref.at[r, c], lambda me, d: out_ref.at[r, me], 2)
    spread("row", lambda t: out_ref.at[r], lambda me, d: out_ref.at[me], 3)


def reduce_all(flat, ident):
    rows, cols = lax.axis_size("row"), lax.axis_size("col")
    part = flat.shape[2:]
    most = max(rows, cols)
    return pl.pallas_call(
        reduce_kernel,
        out_shape=jax.ShapeDtypeStruct(flat.shape, flat.dtype),
        in_specs=[VMEM],
        out_specs=VMEM,
        scratch_shapes=[
            pltpu.VMEM((rows - 1, cols) + part, jnp.float32),
            pltpu.VMEM((cols,) + part, jnp.float32),
            pltpu.VMEM((cols - 1,) + part, jnp.float32),
            pltpu.SemaphoreType.DMA((4, 2, most)),
        ],
        compiler_params=pltpu.CompilerParams(collective_id=ident, has_side_effects=True),
    )(flat)


def half(ref, k, h, t):
    return ref[k, h, pl.ds(t, 1), :]


def walk(lines, tile, blocks, group, start, step):
    def outer(b, carry):
        def inner(j, carry):
            time = b * tile + j
            rising = b * (tile * lines) + j
            falling = (blocks - 1 - b) * (tile * lines) + (tile - 1 - j)
            tokens = [[base + line * tile for line in group] for base in (rising, falling)]
            return step(carry, tokens, time)

        return lax.fori_loop(0, tile, inner, carry, unroll=2)

    return lax.fori_loop(0, blocks, outer, start)


def groups_of(lines):
    size = 2 if lines % 2 == 0 else 1
    return [tuple(range(g, g + size)) for g in range(0, lines, size)]


def fold(ref, k, h, count):
    total = ref[k, h, pl.ds(0, count, stride=SUB), :]
    for s in range(1, SUB):
        total = total + ref[k, h, pl.ds(s, count, stride=SUB), :]
    return total


def softplus(x):
    return jnp.maximum(x, 0.0) + jnp.log1p(jnp.exp(-jnp.abs(x)))


def cross(a, b):
    return lax.dot_general(a, b, (((0,), (0,)), ((), ())), preferred_element_type=jnp.float32)


def back(a, b):
    return lax.dot_general(a, b, (((1,), (1,)), ((), ())), preferred_element_type=jnp.float32)


def block_kernel(
    tile_rows, tile_cols, states, rank,
    embedded_ref, upstream_ref, norm_gain_ref, in_weight_ref, scan_weight_ref, step_weight_ref,
    step_bias_ref, rate_ref, skip_ref, output_gain_ref, output_weight_ref,
    feature_ref, in_grad_ref, scan_grad_ref, stepw_ref, stepb_ref, dr_ref, skip_grad_ref,
    norm_grad_ref, gain_grad_ref, out_grad_ref,
    mixed, gate_grad, turn, along, down, wide, sv, steps, slope, low, hist, eight, pace8, up, dproj, sems,
):
    count, inner = tile_rows * tile_cols, output_weight_ref.shape[0]
    rows, cols = lax.axis_size("row"), lax.axis_size("col")
    eh, nh = inner // LANES, states // SUB
    group = rank + 2 * states
    shapes = ((tile_rows // cols, tile_cols), (tile_cols // rows, tile_rows))
    boxes = (along, down)
    axes = ("col", "row")
    greet(("row", "col"))

    def post(turn_number, pair):
        axis, box = axes[pair], boxes[pair]
        size = lax.axis_size(axis)
        me = lax.axis_index(axis)
        copies = []
        for d in range(1, size):
            target = lax.rem(me + d, size)
            copy = pltpu.make_async_remote_copy(
                src_ref=box.at[2 * turn_number, target],
                dst_ref=box.at[2 * turn_number + 1, me],
                send_sem=sems.at[turn_number, pair, 0, d],
                recv_sem=sems.at[turn_number, pair, 1, d],
                device_id={axis: target},
                device_id_type=MESH,
            )
            copy.start()
            copies.append(copy)
        box[2 * turn_number + 1, me] = box[2 * turn_number, me]
        return copies

    def finish(copies):
        for copy in copies:
            copy.wait()

    def put_home(turn_number, x):
        along[2 * turn_number] = x.reshape(along.shape[1:])
        first = post(turn_number, 0)
        for h in range(eh):
            turn[h] = x[:, h * LANES : (h + 1) * LANES]
        per = tile_cols // rows
        for c in range(tile_cols):
            for h in range(eh):
                down[
                    2 * turn_number, c // per,
                    (c % per) * tile_rows : (c % per + 1) * tile_rows,
                    h * LANES : (h + 1) * LANES,
                ] = turn[h, pl.ds(c, tile_rows, stride=tile_cols), :]
        return first, post(turn_number, 1)

    def take_home(turn_number):
        per = tile_cols // rows
        for c in range(tile_cols):
            for h in range(eh):
                turn[h, pl.ds(c, tile_rows, stride=tile_cols), :] = down[
                    2 * turn_number + 1, c // per,
                    (c % per) * tile_rows : (c % per + 1) * tile_rows,
                    h * LANES : (h + 1) * LANES,
                ]
        here = along[2 * turn_number + 1].reshape(count, inner)
        return here + jnp.concatenate([turn[h] for h in range(eh)], axis=1)

    def lines_in(turn_number, pair):
        return boxes[pair][2 * turn_number + 1].reshape(count, inner)

    def lines_out(turn_number, pair, x):
        boxes[pair][2 * turn_number] = x.reshape(boxes[pair].shape[1:])
        return post(turn_number, pair)

    def rate_of(d, m, h):
        return rate_ref[d, m * SUB : (m + 1) * SUB, h * LANES : (h + 1) * LANES]

    def part(h):
        return slice(h * LANES, (h + 1) * LANES)

    zero = jnp.zeros((SUB, LANES), jnp.float32)

    embedded = embedded_ref[...]
    normed = layer_norm(embedded, norm_gain_ref[...]).astype(jnp.bfloat16)
    mixed[...] = jnp.dot(normed, in_weight_ref[...], preferred_element_type=jnp.float32)
    values = jax.nn.silu(mixed[:, :inner]).astype(jnp.bfloat16).astype(jnp.float32)
    arriving = put_home(0, values)

    leaving = []
    for pair in range(2):
        lines, tile = shapes[pair]
        length = count // lines
        blocks = length // tile
        finish(arriving[pair])
        value = lines_in(0, pair)
        wide_p, sv_p, steps_p, hist_p = wide.at[pair], sv.at[pair], steps.at[pair], hist.at[pair]
        weight = scan_weight_ref[:, 2 * pair * group : 2 * (pair + 1) * group]
        projected = jnp.dot(
            value.astype(jnp.bfloat16), weight, preferred_element_type=jnp.float32
        )
        for k in range(2):
            d = 2 * pair + k
            lowrank = projected[:, k * group : k * group + rank]
            low[d] = lowrank
            before = (
                jnp.dot(
                    lowrank, step_weight_ref[d], precision=HIGHEST,
                    preferred_element_type=jnp.float32,
                )
                + step_bias_ref[d : d + 1, :]
            )
            slope[d] = jax.nn.sigmoid(before)
            pace = softplus(before)
            for h in range(eh):
                steps_p[k, h] = pace[:, part(h)]
                sv_p[k, h] = pace[:, part(h)] * value[:, part(h)]
            for which in range(2):
                for n in range(states):
                    col = k * group + rank + which * states + n
                    wide_p[k, which, pl.ds(n, count, stride=states), :] = jnp.broadcast_to(
                        projected[:, col : col + 1], (count, LANES)
                    )
            for h in range(eh):
                for line in range(lines):
                    at = line * (length + 1) * states
                    hist_p[k, h, at : at + states, :] = jnp.zeros((states, LANES), jnp.float32)
        for lot in groups_of(lines):

            def advance(carry, tokens, time):
                new = []
                i = 0
                for k in range(2):
                    for line, t in zip(lot, tokens[k]):
                        drive = [half(sv_p, k, h, t) for h in range(eh)]
                        pace = [half(steps_p, k, h, t) for h in range(eh)]
                        sums = [None] * eh
                        for m in range(nh):
                            at = pl.ds(pl.multiple_of(t * states + m * SUB, SUB), SUB)
                            slot = (line * (length + 1) + time + 1) * states + m * SUB
                            source = wide_p[k, 0, at, :]
                            probe = wide_p[k, 1, at, :]
                            for h in range(eh):
                                a = jnp.exp2(pace[h] * rate_of(2 * pair + k, m, h))
                                state = a * carry[i] + source * drive[h]
                                i += 1
                                hist_p[k, h, pl.ds(pl.multiple_of(slot, SUB), SUB), :] = state
                                new.append(state)
                                term = probe * state
                                sums[h] = term if sums[h] is None else sums[h] + term
                        for h in range(eh):
                            eight[k, h, pl.ds(pl.multiple_of(t * SUB, SUB), SUB), :] = sums[h]
                return tuple(new)

            walk(lines, tile, blocks, lot, (zero,) * (2 * len(lot) * eh * nh), advance)
        skip = skip_ref[2 * pair : 2 * pair + 1, :] + skip_ref[2 * pair + 1 : 2 * pair + 2, :]
        y = skip * value + jnp.concatenate(
            [fold(eight, 0, h, count) + fold(eight, 1, h, count) for h in range(eh)], axis=1
        )
        leaving.append(lines_out(1, pair, y))
    finish(leaving[0])
    finish(leaving[1])
    total = take_home(1)

    upstream = upstream_ref[...]
    gated, gate_pull = jax.vjp(gate_output, total, mixed[:, inner:], output_gain_ref[...])
    d_gated = back(upstream, output_weight_ref[...])
    d_total, d_gate_in, gain_grad = gate_pull(d_gated)
    arriving = put_home(2, d_total)
    gate_grad[...] = d_gate_in
    gain_grad_ref[...] = gain_grad
    out_grad_ref[...] = cross(gated.astype(jnp.bfloat16), upstream)

    leaving = []
    for pair in range(2):
        lines, tile = shapes[pair]
        length = count // lines
        blocks = length // tile
        finish(arriving[pair])
        g_all = lines_in(2, pair)
        wide_p, sv_p, steps_p, hist_p = wide.at[pair], sv.at[pair], steps.at[pair], hist.at[pair]
        for h in range(eh):
            up[0, h] = g_all[:, part(h)]
        for lot in groups_of(lines):

            def retreat(carry, tokens, time):
                grads, rates = carry
                rates = list(rates)
                new = []
                i = 0
                for k in range(2):
                    for line, t in zip(lot, tokens[1 - k]):
                        drive = [half(sv_p, k, h, t) for h in range(eh)]
                        pace = [half(steps_p, k, h, t) for h in range(eh)]
                        g = [half(up, 0, h, t) for h in range(eh)]
                        dd = [None] * eh
                        dp = [None] * eh
                        for m in range(nh):
                            at = pl.ds(pl.multiple_of(t * states + m * SUB, SUB), SUB)
                            slot = (line * (length + 1) + length - 1 - time) * states + m * SUB
                            earlier = pl.ds(pl.multiple_of(slot, SUB), SUB)
                            current = pl.ds(pl.multiple_of(slot + states, SUB), SUB)
                            source = wide_p[k, 0, at, :]
                            probe = wide_p[k, 1, at, :]
                            flow = None
                            read = None
                            for h in range(eh):
                                rate = rate_of(2 * pair + k, m, h)
                                grad = grads[i] + probe * g[h]
                                i += 1
                                term = grad * drive[h]
                                flow = term if flow is None else flow + term
                                term = g[h] * hist_p[k, h, current, :]
                                read = term if read is None else read + term
                                term = grad * source
                                dd[h] = term if dd[h] is None else dd[h] + term
                                carried = jnp.exp2(pace[h] * rate) * grad
                                q = carried * hist_p[k, h, earlier, :]
                                term = q * rate
                                dp[h] = term if dp[h] is None else dp[h] + term
                                j = (k * nh + m) * eh + h
                                rates[j] = rates[j] + q * pace[h]
                                new.append(carried)
                            wide_p[k, 0, at, :] = flow
                            wide_p[k, 1, at, :] = read
                        for h in range(eh):
                            at8 = pl.ds(pl.multiple_of(t * SUB, SUB), SUB)
                            eight[k, h, at8, :] = dd[h]
                            pace8[k, h, at8, :] = dp[h]
                return (tuple(new), tuple(rates))

            chains = 2 * len(lot) * eh * nh
            unused, rates = walk(
                lines, tile, blocks, lot, ((zero,) * chains, (zero,) * (2 * eh * nh)), retreat
            )
            for k in range(2):
                for m in range(nh):
                    for h in range(eh):
                        place = (2 * pair + k, slice(m * SUB, (m + 1) * SUB), part(h))
                        add = rates[(k * nh + m) * eh + h] * rate_ref[place] * (1.0 / LOG2E)
                        if lot[0] == 0:
                            dr_ref[place] = add
                        else:
                            dr_ref[place] += add
        value = lines_in(0, pair)
        g_all = lines_in(2, pair)
        skip = skip_ref[2 * pair : 2 * pair + 1, :] + skip_ref[2 * pair + 1 : 2 * pair + 2, :]
        dv = skip * g_all
        direct = jnp.sum(g_all * value, axis=0, keepdims=True)
        for k in range(2):
            d = 2 * pair + k
            skip_grad_ref[d : d + 1, :] = direct
            drive = jnp.concatenate([fold(eight, k, h, count) for h in range(eh)], axis=1)
            pace = jnp.concatenate([fold(pace8, k, h, count) for h in range(eh)], axis=1)
            dv = dv + drive * jnp.concatenate([steps_p[k, h] for h in range(eh)], axis=1)
            d_before = (drive * value + pace * (1.0 / LOG2E)) * slope[d]
            stepb_ref[d : d + 1, :] = jnp.sum(d_before, axis=0, keepdims=True)
            stepw_ref[d] = lax.dot_general(
                low[d], d_before, (((0,), (0,)), ((), ())), precision=HIGHEST,
                preferred_element_type=jnp.float32,
            )
            dproj[:, k * group : k * group + rank] = lax.dot_general(
                d_before, step_weight_ref[d], (((1,), (1,)), ((), ())), precision=HIGHEST,
                preferred_element_type=jnp.float32,
            )
            for which in range(2):
                for n in range(states):
                    col = k * group + rank + which * states + n
                    dproj[:, col : col + 1] = jnp.sum(
                        wide_p[k, which, pl.ds(n, count, stride=states), :], axis=-1, keepdims=True
                    )
        d_projected = dproj[...].astype(jnp.bfloat16)
        span = slice(2 * pair * group, 2 * (pair + 1) * group)
        leaving.append(lines_out(3, pair, back(d_projected, scan_weight_ref[:, span]) + dv))
        scan_grad_ref[:, span] = cross(value.astype(jnp.bfloat16), d_projected)
    finish(leaving[0])
    finish(leaving[1])
    d_values = take_home(3)

    d_mixed = jnp.concatenate(
        [d_values * silu_slope(mixed[:, :inner]), gate_grad[...]], axis=1
    ).astype(jnp.bfloat16)
    normed, norm_pull = jax.vjp(layer_norm, embedded_ref[...], norm_gain_ref[...])
    in_grad_ref[...] = cross(normed.astype(jnp.bfloat16), d_mixed)
    d_embedded, norm_grad_ref[...] = norm_pull(back(d_mixed, in_weight_ref[...]))
    feature_ref[...] = (upstream_ref[...].astype(jnp.float32) + d_embedded).astype(jnp.bfloat16)


def local(
    classes, features, cotangent, table, norm_gain, in_weight, scan_weight, step_weight,
    step_bias, decay_log, skip_gain, output_gain, output_weight,
):
    tile_rows, tile_cols, model_width = features.shape
    inner = output_weight.shape[0]
    count = tile_rows * tile_cols
    rows, cols = lax.axis_size("row"), lax.axis_size("col")
    rank = step_weight.shape[1]
    states = decay_log.shape[1]
    group = rank + 2 * states
    eh = inner // LANES
    lines = max(tile_rows // cols, tile_cols // rows)
    grad_scale = float(count * rows * cols) ** (-0.5)
    rate2 = -jnp.exp(decay_log) * LOG2E
    embedded = embed(features, classes, table).reshape(count, model_width)
    f32 = jnp.float32
    shapes = [
        ((count, model_width), jnp.bfloat16),
        (in_weight.shape, f32),
        (scan_weight.shape, f32),
        (step_weight.shape, f32),
        (step_bias.shape, f32),
        (decay_log.shape, f32),
        (skip_gain.shape, f32),
        ((1, model_width), f32),
        ((1, inner), f32),
        (output_weight.shape, f32),
    ]
    scratch = [
        ((count, 2 * inner), f32),
        ((count, inner), f32),
        ((eh, count, LANES), f32),
        ((8, cols, count // cols, inner), f32),
        ((8, rows, count // rows, inner), f32),
        ((2, 2, 2, count * states, LANES), f32),
        ((2, 2, eh, count, LANES), f32),
        ((2, 2, eh, count, LANES), f32),
        ((4, count, inner), f32),
        ((4, count, rank), f32),
        ((2, 2, eh, (count + lines) * states, LANES), f32),
        ((2, eh, count * SUB, LANES), f32),
        ((2, eh, count * SUB, LANES), f32),
        ((1, eh, count, LANES), f32),
        ((count, 2 * group), f32),
    ]
    feature_grad, *grads = pl.pallas_call(
        functools.partial(block_kernel, tile_rows, tile_cols, states, rank),
        out_shape=[jax.ShapeDtypeStruct(*s) for s in shapes],
        in_specs=[VMEM] * 11,
        out_specs=[VMEM] * 10,
        scratch_shapes=[pltpu.VMEM(*s) for s in scratch]
        + [pltpu.SemaphoreType.DMA((4, 2, 2, max(rows, cols)))],
        compiler_params=pltpu.CompilerParams(
            vmem_limit_bytes=BIG, collective_id=1, has_side_effects=True
        ),
    )(
        embedded, cotangent.reshape(count, model_width), norm_gain[None], in_weight, scan_weight,
        step_weight, step_bias, rate2, skip_gain, output_gain[None], output_weight,
    )
    feature_grad = feature_grad.reshape(tile_rows, tile_cols, model_width)
    grads[6], grads[7] = grads[6][0], grads[7][0]
    flat = jnp.concatenate([g.reshape(-1, LANES) for g in grads], axis=0)
    used = flat.shape[0]
    unit = rows * cols * SUB
    padded = -(-used // unit) * unit
    flat = jnp.pad(flat, ((0, padded - used), (0, 0))).reshape(rows, cols, padded // (rows * cols), LANES)
    flat = reduce_all(flat, 2).reshape(padded, LANES) * grad_scale
    summed = []
    place = 0
    for g in grads:
        length = g.size // LANES
        summed.append(flat[place : place + length].reshape(g.shape))
        place += length
    return (feature_grad, *summed)


def solution(mesh):
    in_specs = (P("row", "col"), P("row", "col", None), P("row", "col", None)) + (P(),) * 10
    out_specs = (P("row", "col", None),) + (P(),) * 9
    return jax.shard_map(local, mesh=mesh, in_specs=in_specs, out_specs=out_specs, check_vma=False)
```

```python
import functools
import math

import jax
import jax.numpy as jnp
from jax import lax
from jax.experimental import pallas as pl
from jax.experimental.pallas import tpu as pltpu
from jax.sharding import PartitionSpec as P

EPS = 1e-05
HIGHEST = lax.Precision.HIGHEST
MESH = pl.DeviceIdType.MESH
LANES = 128
SUB = 8
LOG2E = math.log2(math.e)
VMEM = pl.BlockSpec(memory_space=pltpu.VMEM)
BIG = 60 * 1024 * 1024


def layer_norm(rows, gain):
    average = jnp.mean(rows, axis=-1, keepdims=True)
    centred = rows - average
    spread = jnp.mean(centred * centred, axis=-1, keepdims=True)
    return centred * lax.rsqrt(spread + EPS) * gain


def silu_slope(before):
    sigma = jax.nn.sigmoid(before)
    return sigma * (1.0 + before * (1.0 - sigma))


def embed(features, classes, table):
    labels = jnp.arange(table.shape[0], dtype=jnp.int32)
    onehot = (classes[..., None] == labels).astype(jnp.float32)
    lookup = jnp.einsum("hwk,kd->hwd", onehot, table, precision=HIGHEST)
    return features.astype(jnp.float32) + lookup


def gate_output(total, gate_in, output_gain):
    return layer_norm(total, output_gain) * jax.nn.silu(gate_in)


def greet(axes):
    barrier = pltpu.get_barrier_semaphore()
    partners = 0
    for axis in axes:
        count = lax.axis_size(axis)
        me = lax.axis_index(axis)
        for d in range(1, count):
            pl.semaphore_signal(
                barrier, inc=1, device_id={axis: lax.rem(me + d, count)}, device_id_type=MESH
            )
            partners += 1
    pl.semaphore_wait(barrier, partners)


def half(ref, k, h, t):
    return ref[k, h, pl.ds(t, 1), :]


def walk(lines, tile, blocks, group, start, step):
    def outer(b, carry):
        def inner(j, carry):
            time = b * tile + j
            rising = b * (tile * lines) + j
            falling = (blocks - 1 - b) * (tile * lines) + (tile - 1 - j)
            tokens = [[base + line * tile for line in group] for base in (rising, falling)]
            return step(carry, tokens, time)

        return lax.fori_loop(0, tile, inner, carry, unroll=2)

    return lax.fori_loop(0, blocks, outer, start)


def groups_of(lines):
    size = 2 if lines % 2 == 0 else 1
    return [tuple(range(g, g + size)) for g in range(0, lines, size)]


def fold(ref, k, h, count):
    total = ref[k, h, pl.ds(0, count, stride=SUB), :]
    for s in range(1, SUB):
        total = total + ref[k, h, pl.ds(s, count, stride=SUB), :]
    return total


def softplus(x):
    return jnp.maximum(x, 0.0) + jnp.log1p(jnp.exp(-jnp.abs(x)))


def cross(a, b):
    return lax.dot_general(a, b, (((0,), (0,)), ((), ())), preferred_element_type=jnp.float32)


def back(a, b):
    return lax.dot_general(a, b, (((1,), (1,)), ((), ())), preferred_element_type=jnp.float32)


def block_kernel(
    tile_rows, tile_cols, states, rank, grad_scale, tiles,
    embedded_ref, upstream_ref, norm_gain_ref, in_weight_ref, scan_weight_ref, step_weight_ref,
    step_bias_ref, rate_ref, skip_ref, output_gain_ref, output_weight_ref,
    feature_ref, in_grad_ref, scan_grad_ref, stepw_ref, stepb_ref, dr_ref, skip_grad_ref,
    norm_grad_ref, gain_grad_ref, out_grad_ref,
    mixed, gate_grad, turn, along, down, wide, sv, steps, slope, low, hist, eight, pace8, up, dproj, dr_acc,
    mine0, from0, side0, all0, mine1, from1, side1, all1, sems, sumsems,
):
    count, inner = tile_rows * tile_cols, output_weight_ref.shape[0]
    rows, cols = lax.axis_size("row"), lax.axis_size("col")
    eh, nh = inner // LANES, states // SUB
    group = rank + 2 * states
    shapes = ((tile_rows // cols, tile_cols), (tile_cols // rows, tile_rows))
    boxes = (along, down)
    axes = ("col", "row")
    greet(("row", "col"))

    def post(turn_number, pair):
        axis, box = axes[pair], boxes[pair]
        size = lax.axis_size(axis)
        me = lax.axis_index(axis)
        copies = []
        for d in range(1, size):
            target = lax.rem(me + d, size)
            copy = pltpu.make_async_remote_copy(
                src_ref=box.at[2 * turn_number, target],
                dst_ref=box.at[2 * turn_number + 1, me],
                send_sem=sems.at[turn_number, pair, 0, d],
                recv_sem=sems.at[turn_number, pair, 1, d],
                device_id={axis: target},
                device_id_type=MESH,
            )
            copy.start()
            copies.append(copy)
        box[2 * turn_number + 1, me] = box[2 * turn_number, me]
        return copies

    def finish(copies):
        for copy in copies:
            copy.wait()

    def put_home(turn_number, x):
        along[2 * turn_number] = x.reshape(along.shape[1:])
        first = post(turn_number, 0)
        for h in range(eh):
            turn[h] = x[:, h * LANES : (h + 1) * LANES]
        per = tile_cols // rows
        for c in range(tile_cols):
            for h in range(eh):
                down[
                    2 * turn_number, c // per,
                    (c % per) * tile_rows : (c % per + 1) * tile_rows,
                    h * LANES : (h + 1) * LANES,
                ] = turn[h, pl.ds(c, tile_rows, stride=tile_cols), :]
        return first, post(turn_number, 1)

    def take_home(turn_number):
        per = tile_cols // rows
        for c in range(tile_cols):
            for h in range(eh):
                turn[h, pl.ds(c, tile_rows, stride=tile_cols), :] = down[
                    2 * turn_number + 1, c // per,
                    (c % per) * tile_rows : (c % per + 1) * tile_rows,
                    h * LANES : (h + 1) * LANES,
                ]
        here = along[2 * turn_number + 1].reshape(count, inner)
        return here + jnp.concatenate([turn[h] for h in range(eh)], axis=1)

    def lines_in(turn_number, pair):
        return boxes[pair][2 * turn_number + 1].reshape(count, inner)

    def lines_out(turn_number, pair, x):
        boxes[pair][2 * turn_number] = x.reshape(boxes[pair].shape[1:])
        return post(turn_number, pair)

    def rate_of(d, m, h):
        return rate_ref[d, m * SUB : (m + 1) * SUB, h * LANES : (h + 1) * LANES]

    def part(h):
        return slice(h * LANES, (h + 1) * LANES)

    zero = jnp.zeros((SUB, LANES), jnp.float32)

    sums = ((mine0, from0, side0, all0), (mine1, from1, side1, all1))
    fill = [0, 0]

    def put(lot, x):
        mine = sums[lot][0]
        per = mine.shape[1] // SUB
        for i in range(x.shape[0] // SUB):
            tile = fill[lot]
            at = (tile % per) * SUB
            mine[tile // per, at : at + SUB, :] = x[i * SUB : (i + 1) * SUB]
            fill[lot] += 1

    def put_wide(lot, x):
        for h in range(x.shape[1] // LANES):
            put(lot, x[:, h * LANES : (h + 1) * LANES])

    taken = [0, 0]

    def take(lot, height):
        full = sums[lot][3]
        per = full.shape[1] // SUB
        out = []
        for i in range(height // SUB):
            tile = taken[lot]
            at = (tile % per) * SUB
            out.append(full[tile // per, at : at + SUB, :])
            taken[lot] += 1
        return jnp.concatenate(out, axis=0) * grad_scale

    def take_wide(lot, height, width):
        return jnp.concatenate([take(lot, height) for h in range(width // LANES)], axis=1)

    def pad_rows(*rows_in):
        missing = -len(rows_in) % SUB
        return jnp.concatenate(list(rows_in) + [jnp.zeros((missing, LANES), jnp.float32)], axis=0)

    def pad_lot(lot):
        while fill[lot] < tiles[lot]:
            put(lot, zero)

    def spread(lot, phase, axis, source, result):
        size = lax.axis_size(axis)
        me = lax.axis_index(axis)
        copies = []
        for d in range(1, size):
            target = lax.rem(me + d, size)
            copy = pltpu.make_async_remote_copy(
                src_ref=source(target),
                dst_ref=result(me, d),
                send_sem=sumsems.at[lot, phase, 0, d],
                recv_sem=sumsems.at[lot, phase, 1, d],
                device_id={axis: target},
                device_id_type=MESH,
            )
            copy.start()
            copies.append(copy)
        return copies

    def sum_scatter(lot):
        mine, other, side, full = sums[lot]
        pad_lot(lot)
        return spread(lot, 0, "row", lambda t: mine.at[t], lambda me, d: other.at[d - 1])

    def sum_across(lot, copies):
        mine, other, side, full = sums[lot]
        finish(copies)
        acc = mine[lax.axis_index("row")]
        for d in range(rows - 1):
            acc = acc + other[d]
        me = lax.axis_index("col")
        side[me] = acc
        return spread(lot, 1, "col", lambda t: side.at[me], lambda m, d: side.at[m])

    def sum_gather(lot, copies):
        mine, other, side, full = sums[lot]
        finish(copies)
        acc = side[0]
        for d in range(1, cols):
            acc = acc + side[d]
        me = lax.axis_index("row")
        full[me] = acc
        return spread(lot, 2, "row", lambda t: full.at[me], lambda m, d: full.at[m])

    embedded = embedded_ref[...]
    normed = layer_norm(embedded, norm_gain_ref[...]).astype(jnp.bfloat16)
    mixed[...] = jnp.dot(normed, in_weight_ref[...], preferred_element_type=jnp.float32)
    values = jax.nn.silu(mixed[:, :inner]).astype(jnp.bfloat16).astype(jnp.float32)
    arriving = put_home(0, values)

    leaving = []
    for pair in range(2):
        lines, tile = shapes[pair]
        length = count // lines
        blocks = length // tile
        finish(arriving[pair])
        value = lines_in(0, pair)
        wide_p, sv_p, steps_p, hist_p = wide.at[pair], sv.at[pair], steps.at[pair], hist.at[pair]
        weight = scan_weight_ref[:, 2 * pair * group : 2 * (pair + 1) * group]
        projected = jnp.dot(
            value.astype(jnp.bfloat16), weight, preferred_element_type=jnp.float32
        )
        for k in range(2):
            d = 2 * pair + k
            lowrank = projected[:, k * group : k * group + rank]
            low[d] = lowrank
            before = (
                jnp.dot(
                    lowrank, step_weight_ref[d], precision=HIGHEST,
                    preferred_element_type=jnp.float32,
                )
                + step_bias_ref[d : d + 1, :]
            )
            slope[d] = jax.nn.sigmoid(before)
            pace = softplus(before)
            for h in range(eh):
                steps_p[k, h] = pace[:, part(h)]
                sv_p[k, h] = pace[:, part(h)] * value[:, part(h)]
            for which in range(2):
                for n in range(states):
                    col = k * group + rank + which * states + n
                    wide_p[k, which, pl.ds(n, count, stride=states), :] = jnp.broadcast_to(
                        projected[:, col : col + 1], (count, LANES)
                    )
            for h in range(eh):
                for line in range(lines):
                    at = line * (length + 1) * states
                    hist_p[k, h, at : at + states, :] = jnp.zeros((states, LANES), jnp.float32)
        for lot in groups_of(lines):

            def advance(carry, tokens, time):
                new = []
                i = 0
                for k in range(2):
                    for line, t in zip(lot, tokens[k]):
                        drive = [half(sv_p, k, h, t) for h in range(eh)]
                        pace = [half(steps_p, k, h, t) for h in range(eh)]
                        sums = [None] * eh
                        for m in range(nh):
                            at = pl.ds(pl.multiple_of(t * states + m * SUB, SUB), SUB)
                            slot = (line * (length + 1) + time + 1) * states + m * SUB
                            source = wide_p[k, 0, at, :]
                            probe = wide_p[k, 1, at, :]
                            for h in range(eh):
                                a = jnp.exp2(pace[h] * rate_of(2 * pair + k, m, h))
                                state = a * carry[i] + source * drive[h]
                                i += 1
                                hist_p[k, h, pl.ds(pl.multiple_of(slot, SUB), SUB), :] = state
                                new.append(state)
                                term = probe * state
                                sums[h] = term if sums[h] is None else sums[h] + term
                        for h in range(eh):
                            eight[k, h, pl.ds(pl.multiple_of(t * SUB, SUB), SUB), :] = sums[h]
                return tuple(new)

            walk(lines, tile, blocks, lot, (zero,) * (2 * len(lot) * eh * nh), advance)
        skip = skip_ref[2 * pair : 2 * pair + 1, :] + skip_ref[2 * pair + 1 : 2 * pair + 2, :]
        y = skip * value + jnp.concatenate(
            [fold(eight, 0, h, count) + fold(eight, 1, h, count) for h in range(eh)], axis=1
        )
        leaving.append(lines_out(1, pair, y))
    finish(leaving[0])
    finish(leaving[1])
    total = take_home(1)

    upstream = upstream_ref[...]
    gated, gate_pull = jax.vjp(gate_output, total, mixed[:, inner:], output_gain_ref[...])
    d_gated = back(upstream, output_weight_ref[...])
    d_total, d_gate_in, gain_grad = gate_pull(d_gated)
    arriving = put_home(2, d_total)
    gate_grad[...] = d_gate_in
    put(0, pad_rows(*[gain_grad[:, part(h)] for h in range(eh)]))
    put_wide(0, cross(gated.astype(jnp.bfloat16), upstream))

    leaving = []
    for pair in range(2):
        lines, tile = shapes[pair]
        length = count // lines
        blocks = length // tile
        finish(arriving[pair])
        g_all = lines_in(2, pair)
        wide_p, sv_p, steps_p, hist_p = wide.at[pair], sv.at[pair], steps.at[pair], hist.at[pair]
        for h in range(eh):
            up[0, h] = g_all[:, part(h)]
        for lot in groups_of(lines):

            def retreat(carry, tokens, time):
                grads, rates = carry
                rates = list(rates)
                new = []
                i = 0
                for k in range(2):
                    for line, t in zip(lot, tokens[1 - k]):
                        drive = [half(sv_p, k, h, t) for h in range(eh)]
                        pace = [half(steps_p, k, h, t) for h in range(eh)]
                        g = [half(up, 0, h, t) for h in range(eh)]
                        dd = [None] * eh
                        dp = [None] * eh
                        for m in range(nh):
                            at = pl.ds(pl.multiple_of(t * states + m * SUB, SUB), SUB)
                            slot = (line * (length + 1) + length - 1 - time) * states + m * SUB
                            earlier = pl.ds(pl.multiple_of(slot, SUB), SUB)
                            current = pl.ds(pl.multiple_of(slot + states, SUB), SUB)
                            source = wide_p[k, 0, at, :]
                            probe = wide_p[k, 1, at, :]
                            flow = None
                            read = None
                            for h in range(eh):
                                rate = rate_of(2 * pair + k, m, h)
                                grad = grads[i] + probe * g[h]
                                i += 1
                                term = grad * drive[h]
                                flow = term if flow is None else flow + term
                                term = g[h] * hist_p[k, h, current, :]
                                read = term if read is None else read + term
                                term = grad * source
                                dd[h] = term if dd[h] is None else dd[h] + term
                                carried = jnp.exp2(pace[h] * rate) * grad
                                q = carried * hist_p[k, h, earlier, :]
                                term = q * rate
                                dp[h] = term if dp[h] is None else dp[h] + term
                                j = (k * nh + m) * eh + h
                                rates[j] = rates[j] + q * pace[h]
                                new.append(carried)
                            wide_p[k, 0, at, :] = flow
                            wide_p[k, 1, at, :] = read
                        for h in range(eh):
                            at8 = pl.ds(pl.multiple_of(t * SUB, SUB), SUB)
                            eight[k, h, at8, :] = dd[h]
                            pace8[k, h, at8, :] = dp[h]
                return (tuple(new), tuple(rates))

            chains = 2 * len(lot) * eh * nh
            unused, rates = walk(
                lines, tile, blocks, lot, ((zero,) * chains, (zero,) * (2 * eh * nh)), retreat
            )
            for k in range(2):
                for m in range(nh):
                    for h in range(eh):
                        place = (2 * pair + k, slice(m * SUB, (m + 1) * SUB), part(h))
                        add = rates[(k * nh + m) * eh + h] * rate_ref[place] * (1.0 / LOG2E)
                        if lot[0] == 0:
                            dr_acc[place] = add
                        else:
                            dr_acc[place] += add
        value = lines_in(0, pair)
        g_all = lines_in(2, pair)
        skip = skip_ref[2 * pair : 2 * pair + 1, :] + skip_ref[2 * pair + 1 : 2 * pair + 2, :]
        dv = skip * g_all
        direct = jnp.sum(g_all * value, axis=0, keepdims=True)
        small = [direct[:, part(h)] for h in range(eh)]
        for k in range(2):
            d = 2 * pair + k
            drive = jnp.concatenate([fold(eight, k, h, count) for h in range(eh)], axis=1)
            pace = jnp.concatenate([fold(pace8, k, h, count) for h in range(eh)], axis=1)
            dv = dv + drive * jnp.concatenate([steps_p[k, h] for h in range(eh)], axis=1)
            d_before = (drive * value + pace * (1.0 / LOG2E)) * slope[d]
            bias_sum = jnp.sum(d_before, axis=0, keepdims=True)
            small += [bias_sum[:, part(h)] for h in range(eh)]
            put_wide(
                pair,
                lax.dot_general(
                    low[d], d_before, (((0,), (0,)), ((), ())), precision=HIGHEST,
                    preferred_element_type=jnp.float32,
                ),
            )
            put_wide(pair, dr_acc[d])
            dproj[:, k * group : k * group + rank] = lax.dot_general(
                d_before, step_weight_ref[d], (((1,), (1,)), ((), ())), precision=HIGHEST,
                preferred_element_type=jnp.float32,
            )
            lane = lax.broadcasted_iota(jnp.int32, (LANES, 2 * states), 1)
            flow = None
            for j in range(2 * states):
                x = wide_p[k, j // states, pl.ds(j % states, count, stride=states), :]
                pick = (lane == j).astype(jnp.bfloat16)
                term = jnp.dot(x.astype(jnp.bfloat16), pick, preferred_element_type=jnp.float32)
                flow = term if flow is None else flow + term
            dproj[:, k * group + rank : (k + 1) * group] = flow
        d_projected = dproj[...].astype(jnp.bfloat16)
        span = slice(2 * pair * group, 2 * (pair + 1) * group)
        leaving.append(lines_out(3, pair, back(d_projected, scan_weight_ref[:, span]) + dv))
        put(pair, pad_rows(*small))
        put_wide(pair, cross(d_projected, value.astype(jnp.bfloat16)))
        if pair == 0:
            early = sum_scatter(0)
        else:
            early = sum_across(0, early)
    finish(leaving[0])
    finish(leaving[1])
    d_values = take_home(3)
    early = sum_gather(0, early)

    d_mixed = jnp.concatenate(
        [d_values * silu_slope(mixed[:, :inner]), gate_grad[...]], axis=1
    ).astype(jnp.bfloat16)
    normed, norm_pull = jax.vjp(layer_norm, embedded_ref[...], norm_gain_ref[...])
    put_wide(1, cross(normed.astype(jnp.bfloat16), d_mixed))
    d_embedded, norm_grad = norm_pull(back(d_mixed, in_weight_ref[...]))
    put(1, pad_rows(norm_grad))
    late = sum_scatter(1)
    feature_ref[...] = (upstream_ref[...].astype(jnp.float32) + d_embedded).astype(jnp.bfloat16)
    late = sum_across(1, late)
    finish(early)
    late = sum_gather(1, late)

    def take_pair(pair):
        for d in (2 * pair, 2 * pair + 1):
            stepw_ref[d] = take_wide(pair, rank, inner)
            dr_ref[d] = take_wide(pair, states, inner)
        small = take(pair, -(-3 * eh // SUB) * SUB)
        for h in range(eh):
            for k in range(2):
                d = 2 * pair + k
                skip_grad_ref[d : d + 1, part(h)] = small[h : h + 1]
                stepb_ref[d : d + 1, part(h)] = small[(k + 1) * eh + h : (k + 1) * eh + h + 1]
        span = slice(2 * pair * group, 2 * (pair + 1) * group)
        scan_grad_ref[:, span] = take_wide(pair, 2 * group, inner).T

    small = take(0, SUB)
    for h in range(eh):
        gain_grad_ref[:, part(h)] = small[h : h + 1]
    out_grad_ref[...] = take_wide(0, inner, out_grad_ref.shape[1])
    take_pair(0)
    finish(late)
    take_pair(1)
    in_grad_ref[...] = take_wide(1, in_grad_ref.shape[0], in_grad_ref.shape[1])
    norm_grad_ref[...] = take(1, SUB)[0:1]


def local(
    classes, features, cotangent, table, norm_gain, in_weight, scan_weight, step_weight,
    step_bias, decay_log, skip_gain, output_gain, output_weight,
):
    tile_rows, tile_cols, model_width = features.shape
    inner = output_weight.shape[0]
    count = tile_rows * tile_cols
    rows, cols = lax.axis_size("row"), lax.axis_size("col")
    rank = step_weight.shape[1]
    states = decay_log.shape[1]
    group = rank + 2 * states
    eh = inner // LANES
    lines = max(tile_rows // cols, tile_cols // rows)
    grad_scale = float(count * rows * cols) ** (-0.5)
    rate2 = -jnp.exp(decay_log) * LOG2E
    embedded = embed(features, classes, table).reshape(count, model_width)
    f32 = jnp.float32
    shapes = [
        ((count, model_width), jnp.bfloat16),
        (in_weight.shape, f32),
        (scan_weight.shape, f32),
        (step_weight.shape, f32),
        (step_bias.shape, f32),
        (decay_log.shape, f32),
        (skip_gain.shape, f32),
        ((1, model_width), f32),
        ((1, inner), f32),
        (output_weight.shape, f32),
    ]
    scratch = [
        ((count, 2 * inner), f32),
        ((count, inner), f32),
        ((eh, count, LANES), f32),
        ((8, cols, count // cols, inner), f32),
        ((8, rows, count // rows, inner), f32),
        ((2, 2, 2, count * states, LANES), f32),
        ((2, 2, eh, count, LANES), f32),
        ((2, 2, eh, count, LANES), f32),
        ((4, count, inner), f32),
        ((4, count, rank), f32),
        ((2, 2, eh, (count + lines) * states, LANES), f32),
        ((2, eh, count * SUB, LANES), f32),
        ((2, eh, count * SUB, LANES), f32),
        ((1, eh, count, LANES), f32),
        ((count, 2 * group), f32),
        (decay_log.shape, f32),
    ]
    pair_tiles = eh * (2 * rank + 2 * states + 2 * group) // SUB + -(-3 * eh // SUB)
    least = (
        1 + inner * model_width // (LANES * SUB) + pair_tiles,
        1 + in_weight.size // (LANES * SUB) + pair_tiles,
    )
    tiles = tuple(-(-t // rows) * rows for t in least)
    for lot in range(2):
        chunk = (tiles[lot] // rows * SUB, LANES)
        scratch += [((rows,) + chunk, f32), ((rows - 1,) + chunk, f32), ((cols,) + chunk, f32), ((rows,) + chunk, f32)]
    feature_grad, *grads = pl.pallas_call(
        functools.partial(block_kernel, tile_rows, tile_cols, states, rank, grad_scale, tiles),
        out_shape=[jax.ShapeDtypeStruct(*s) for s in shapes],
        in_specs=[VMEM] * 11,
        out_specs=[VMEM] * 10,
        scratch_shapes=[pltpu.VMEM(*s) for s in scratch]
        + [
            pltpu.SemaphoreType.DMA((4, 2, 2, max(rows, cols))),
            pltpu.SemaphoreType.DMA((2, 3, 2, max(rows, cols))),
        ],
        compiler_params=pltpu.CompilerParams(
            vmem_limit_bytes=BIG, collective_id=1, has_side_effects=True
        ),
    )(
        embedded, cotangent.reshape(count, model_width), norm_gain[None], in_weight, scan_weight,
        step_weight, step_bias, rate2, skip_gain, output_gain[None], output_weight,
    )
    feature_grad = feature_grad.reshape(tile_rows, tile_cols, model_width)
    grads[6], grads[7] = grads[6][0], grads[7][0]
    return (feature_grad, *grads)


def solution(mesh):
    in_specs = (P("row", "col"), P("row", "col", None), P("row", "col", None)) + (P(),) * 10
    out_specs = (P("row", "col", None),) + (P(),) * 9
    return jax.shard_map(local, mesh=mesh, in_specs=in_specs, out_specs=out_specs, check_vma=False)
```
